512 devices in a mesh: seq: 32 (over y, x, core), head: 16 (over z).
Axes of the slice: x: 4, y: 4, z: 16, core: 2. Of those that a mesh axis runs over, the one named last changes fastest.
Arguments:
- queries: bfloat16 [16384, 8192], P('seq', 'head'), may hold values from -0.9 to 0.9
- keys: bfloat16 [16384, 8192], P('seq', 'head'), may hold values from -0.9 to 0.9
- values: bfloat16 [16384, 8192], P('seq', 'head'), may hold values from -0.9 to 0.9
- grad_out: bfloat16 [16384, 8192], P('seq', 'head'), may hold values from -0.9 to 0.9
- rates: float32 [64], P('head'), may hold values from 3.0517578e-05 to 0.04
- doc_lengths: int32 [8], replicated, may hold values from 1 to 12288, 16384 in all
Outputs:
- grad_queries: bfloat16 [16384, 8192], P(('seq', 'head'))
- grad_keys: bfloat16 [16384, 8192], P(('seq', 'head'))
- grad_values: bfloat16 [16384, 8192], P(('seq', 'head'))
The draws below stay inside these ranges and needn't reach their ends.
Inputs may be any that keep to these rules, and one draw needn't show every extreme that they name: `doc_lengths`: lengths of the completions in order, summing to 16384; the longest has exactly 12288 tokens.
All inputs are finite; a program needn't handle non-finite values.
Results may differ from the reference program's by a relative error of at most 0.001.
The reference program's roundings to bfloat16 on the way count: a program that leaves them out, or rounds other values in their place, can miss the bound.
Values may be sent and summed in bfloat16 or wider, within the bound.
No kernel may reach another device: no remote copies, remote signals or barrier semaphores. Data moves between devices by JAX's collectives and lax.ppermute only.
A program may use at most 64 MiB of HBM per device.

```python
import math
import jax
import jax.numpy as jnp
import numpy as np
from jax import lax

H = 64
HD = 128
TOK_DEV = 512
DOCS = 8
TOKENS = 16384
MOST = 12288
INNER = 8192


def loud_blocks(key, salt):
    own_key = jax.random.fold_in(key, salt)
    entry_key, factor_key = jax.random.split(own_key)
    entries = jnp.clip(0.15 * jax.random.normal(entry_key, (TOKENS, INNER), jnp.float32), -0.9, 0.9)
    blocks = TOKENS // TOK_DEV
    factors = jnp.exp(-3.4 * jax.random.uniform(factor_key, (blocks, 1, 1), jnp.float32))
    shaped = entries.reshape(blocks, TOK_DEV, INNER) * factors
    return shaped.reshape(TOKENS, INNER).astype(jnp.bfloat16)


def draw_queries(key, part):
    return loud_blocks(key, 101)


def draw_keys(key, part):
    return loud_blocks(key, 202)


def draw_values(key, part):
    return loud_blocks(key, 303)


def draw_grad_out(key, part):
    return loud_blocks(key, 404)


def block_levels(key, shape, cuts, least, high):
    gain = 1.0
    for position, parts in cuts:
        draws = jax.random.uniform(jax.random.fold_in(jax.random.fold_in(key, 6), position), (parts,), jnp.float32, least / len(cuts), high / len(cuts))
        gain = gain * jnp.repeat(jnp.exp(draws), shape[position] // parts).reshape((-1,) + (1,) * (len(shape) - 1 - position))
    return gain


def split_up(count, total, reach, skew):
    portions = [(1 << 20) // math.isqrt(rank ** skew) + 1 for rank in range(2, count + 1)]
    rest, given = total - reach - (count - 1), [1] * (count - 1)
    while rest > 0:
        free = [i for i in range(count - 1) if given[i] < reach]
        mass, left = sum([portions[i] for i in free]), rest
        for i in free:
            more = min(reach - given[i], max(1, left * portions[i] // mass), rest)
            given[i] = given[i] + more
            rest = rest - more
    return np.array([reach] + given)


def ragged(key, count, total, reach, slope):
    if count == 2:
        one = jax.random.randint(key, (), max(1, total - reach), min(reach, total - 1) + 1)
        return jnp.stack([one, total - one])
    sizes = jnp.asarray(split_up(count, total, reach, slope), jnp.int32)
    twos = (count - 1) // 2
    giver, receiver = sizes[1:1 + 2 * twos:2], sizes[2:2 + 2 * twos:2]
    room = jnp.minimum(giver - 1, reach - receiver)
    passed = jax.random.randint(jax.random.fold_in(key, 1), (twos,), 0, 1 << 20) % (room + 1)
    sizes = sizes.at[1:1 + 2 * twos:2].set(giver - passed).at[2:2 + 2 * twos:2].set(receiver + passed)
    return sizes[jax.random.permutation(jax.random.fold_in(key, 2), count)]


def setup_inputs(seed: int = 0) -> dict:
    streams_of = jax.random.split(jax.random.key(seed), 7)
    queries = draw_queries(jax.random.fold_in(streams_of[6], 71), 0)
    keys = draw_keys(jax.random.fold_in(streams_of[6], 71), 0)
    values = draw_values(jax.random.fold_in(streams_of[6], 71), 0)
    grad_out = draw_grad_out(jax.random.fold_in(streams_of[6], 71), 0)
    rates = jnp.clip(jnp.exp(math.log(0.04) - 7.178332 * jax.random.uniform(streams_of[4], (H,), jnp.float32) ** block_levels(streams_of[4], (H,), ((0, 16),), -0.2, 0.2)), 3.0517578125e-05, 0.04)
    doc_lengths = ragged(streams_of[5], DOCS, TOKENS, MOST, 2).astype(jnp.int32)
    return dict(queries=queries, keys=keys, values=values, grad_out=grad_out, rates=rates, doc_lengths=doc_lengths)


def seg_ids(doc_lengths, positions):
    starts = jnp.cumsum(doc_lengths, dtype=jnp.int32) - doc_lengths
    inside = (starts[None, :] <= positions[:, None]).astype(jnp.int32)
    return jnp.sum(inside, axis=1, dtype=jnp.int32) - 1


def rounded(array):
    return lax.optimization_barrier(array.astype(jnp.bfloat16)).astype(jnp.float32)


def block_grads(query_rows, key_rows, value_rows, grad_rows, segment, seg_prev, seg_next, state_in, back_in, rates):
    length = query_rows.shape[0]
    offsets = jnp.arange(length, dtype=jnp.float32)
    distance = offsets[:, None] - offsets[None, :]
    allowed = (segment[:, None] == segment[None, :]) & (distance >= 0)
    decayed = jnp.where(allowed[None], jnp.exp(-rates[:, None, None] * jnp.maximum(distance, 0.0)[None]), 0.0)
    query_full = query_rows.astype(jnp.float32)
    key_full = key_rows.astype(jnp.float32)
    value_full = value_rows.astype(jnp.float32)
    grad_full = grad_rows.astype(jnp.float32)
    scores_gv = jnp.einsum("the,uhe->htu", grad_full, value_full)
    scores_qk = jnp.einsum("thd,uhd->htu", query_full, key_full)
    weights_p = rounded(decayed * scores_gv)
    weights_a = rounded(decayed * scores_qk)
    local_q = jnp.einsum("htu,uhd->thd", weights_p, key_full)
    local_k = jnp.einsum("htu,thd->uhd", weights_p, query_full)
    local_v = jnp.einsum("htu,the->uhe", weights_a, grad_full)
    factor_in = jnp.where((segment == seg_prev)[:, None], jnp.exp(-rates[None, :] * (offsets + 1.0)[:, None]), 0.0)
    factor_back = jnp.where((segment == seg_next)[:, None], jnp.exp(-rates[None, :] * (length - offsets)[:, None]), 0.0)
    state_b = rounded(state_in)
    back_b = rounded(back_in)
    outer_q = jnp.einsum("the,hde->thd", grad_full, state_b) * factor_in[:, :, None]
    outer_k = jnp.einsum("the,hde->thd", value_full, back_b) * factor_back[:, :, None]
    outer_v = jnp.einsum("thd,hde->the", key_full, back_b) * factor_back[:, :, None]
    return ((local_q + outer_q).astype(jnp.bfloat16), (local_k + outer_k).astype(jnp.bfloat16), (local_v + outer_v).astype(jnp.bfloat16))


def reference(queries, keys, values, grad_out, rates, doc_lengths):
    length = TOK_DEV
    blocks = TOKENS // TOK_DEV
    query_blk = queries.reshape(blocks, length, H, HD)
    key_blk = keys.reshape(blocks, length, H, HD)
    value_blk = values.reshape(blocks, length, H, HD)
    grad_blk = grad_out.reshape(blocks, length, H, HD)
    positions = jnp.arange(TOKENS, dtype=jnp.int32)
    segment = seg_ids(doc_lengths, positions).reshape(blocks, length)
    firsts = jnp.arange(blocks, dtype=jnp.int32) * length
    seg_prev = seg_ids(doc_lengths, firsts - 1)
    seg_next = seg_ids(doc_lengths, firsts + length)
    keep_fwd = (segment[:, -1] == seg_prev).astype(jnp.float32)
    keep_bwd = (segment[:, 0] == seg_next).astype(jnp.float32)
    decay = jnp.exp(-rates * length)
    offsets = jnp.arange(length, dtype=jnp.float32)

    def forward_step(carry, items):
        key_rows, value_rows, seg_rows, keep = items
        weight = jnp.where((seg_rows == seg_rows[-1])[:, None], jnp.exp(-rates[None, :] * (length - 1.0 - offsets)[:, None]), 0.0)
        weighted = rounded(key_rows.astype(jnp.float32) * weight[:, :, None])
        summary = jnp.einsum("uhd,uhe->hde", weighted, value_rows.astype(jnp.float32))
        return keep * decay[:, None, None] * carry + summary, carry

    def backward_step(carry, items):
        query_rows, grad_rows, seg_rows, keep = items
        weight = jnp.where((seg_rows == seg_rows[0])[:, None], jnp.exp(-rates[None, :] * offsets[:, None]), 0.0)
        weighted = rounded(query_rows.astype(jnp.float32) * weight[:, :, None])
        summary = jnp.einsum("thd,the->hde", weighted, grad_rows.astype(jnp.float32))
        return keep * decay[:, None, None] * carry + summary, carry

    zero_state = jnp.zeros((H, HD, HD), jnp.float32)
    _, states_in = lax.scan(forward_step, zero_state, (key_blk, value_blk, segment, keep_fwd))
    _, backs_in = lax.scan(backward_step, zero_state, (query_blk, grad_blk, segment, keep_bwd), reverse=True)

    def one_block(items):
        query_rows, key_rows, value_rows, grad_rows, seg_rows, prev_one, next_one, state_one, back_one = items
        return block_grads(query_rows, key_rows, value_rows, grad_rows, seg_rows, prev_one, next_one, state_one, back_one, rates)

    grad_q, grad_k, grad_v = lax.map(one_block, (query_blk, key_blk, value_blk, grad_blk, segment, seg_prev, seg_next, states_in, backs_in))
    return (grad_q.reshape(TOKENS, INNER), grad_k.reshape(TOKENS, INNER), grad_v.reshape(TOKENS, INNER))
```

```python
import functools

import jax
import jax.numpy as jnp
from jax import lax
from jax.experimental import pallas as pl
from jax.experimental.pallas import tpu as pltpu
from jax.sharding import PartitionSpec as P

BF16 = jnp.bfloat16
F32 = jnp.float32
FAR = 1 << 30


def doc_starts(docs_ref, docs):
    starts = [jnp.int32(0)]
    for i in range(docs - 1):
        starts.append(starts[-1] + docs_ref[i])
    return starts


def last_start(starts, position):
    found = jnp.int32(-1)
    for s in starts:
        found = jnp.maximum(found, jnp.where(s <= position, s, -1))
    return found


def next_start(starts, position):
    found = jnp.int32(FAR)
    for s in starts:
        found = jnp.minimum(found, jnp.where(s > position, s, FAR))
    return found


def dot(a, b, da, db):
    return lax.dot_general(a, b, (((da,), (db,)), ((), ())), preferred_element_type=F32)


def fetch(refs, buffer, sems, hd, head):
    return [
        pltpu.make_async_copy(
            ref.at[:, pl.ds(head * hd, hd)], buffer.at[i, head], sems.at[i, head]
        )
        for i, ref in enumerate(refs)
    ]


def summary_kernel(
    length, docs, heads, rates_ref, docs_ref, k_ref, v_ref, q_ref, g_ref, out_ref, held, sems
):
    hd = out_ref.shape[-1]
    copies = [fetch((k_ref, v_ref, q_ref, g_ref), held, sems, hd, h) for h in range(heads)]
    for group in copies:
        for copy in group:
            copy.start()
    first = lax.axis_index("seq") * length
    starts = doc_starts(docs_ref, docs)
    from_here = last_start(starts, first + length - 1) - first
    until_here = next_start(starts, first) - first
    token = lax.broadcasted_iota(jnp.int32, (1, length), 1)
    offset = token.astype(F32)
    for h in range(heads):
        rate = rates_ref[h]
        weight_k = jnp.where(token >= from_here, jnp.exp(-rate * (length - 1.0 - offset)), 0.0)
        weight_q = jnp.where(token < until_here, jnp.exp(-rate * offset), 0.0)
        for way, weight in enumerate((weight_k, weight_q)):
            copies[h][2 * way].wait()
            weighted = (held[2 * way, h].T.astype(F32) * weight).astype(BF16)
            copies[h][2 * way + 1].wait()
            out_ref[way, h] = dot(weighted, held[2 * way + 1, h], 1, 0)


def local_kernel(
    length, docs, heads, blocks,
    rates_ref, docs_ref, q_ref, k_ref, v_ref, g_ref,
    lq_ref, lk_ref, lv_ref, keep_ref,
):
    head = pl.program_id(0)
    rate = rates_ref[head]
    first = lax.axis_index("seq") * length
    starts = doc_starts(docs_ref, docs)
    t = lax.broadcasted_iota(jnp.int32, (length, length), 0)
    u = lax.broadcasted_iota(jnp.int32, (length, length), 1)
    column = lax.broadcasted_iota(jnp.int32, (length, 1), 0)
    own = jnp.full((length, 1), -FAR, jnp.int32)
    for s in starts:
        here = s - first
        own = jnp.maximum(own, jnp.where(column >= here, here, -FAR))
    distance = (t - u).astype(F32)
    allowed = (u >= own) & (u <= t)
    decayed = jnp.where(allowed, jnp.exp(-rate * jnp.maximum(distance, 0.0)), 0.0)
    q, k, v, g = q_ref[...], k_ref[...], v_ref[...], g_ref[...]
    weights_p = (decayed * dot(g, v, 1, 1)).astype(BF16)
    lq_ref[...] = dot(weights_p, k, 1, 0)
    lk_ref[...] = dot(weights_p, q, 0, 0)
    weights_a = (decayed * dot(q, k, 1, 1)).astype(BF16)
    lv_ref[...] = dot(weights_a, g, 0, 0)

    @pl.when(head == 0)
    def _():
        me = lax.axis_index("seq")
        per_way = blocks // 2
        backward = me // per_way
        mine = rates_ref[(me % per_way) // (per_way // heads)]
        low = lax.broadcasted_iota(jnp.int32, keep_ref.shape, 0) * length + backward
        broken = low < 0
        for s in starts:
            broken = broken | ((s >= low) & (s < low + length))
        decay = jnp.exp(jnp.full(keep_ref.shape, -mine * length, F32))
        keep_ref[...] = jnp.where(broken, 0.0, decay)


def scan_kernel(blocks, keep_ref, in_ref, out_ref):
    backward = lax.axis_index("seq") // (blocks // 2)
    carry = jnp.zeros(in_ref.shape[1:], F32)
    for i in range(blocks):
        j = jnp.where(backward == 1, blocks - 1 - i, i)
        out_ref[j] = carry.astype(BF16)
        carry = keep_ref[pl.ds(j, 1), :] * carry + in_ref[j]


def final_kernel(
    length, docs, heads,
    rates_ref, docs_ref, g_ref, v_ref, k_ref, lq_ref, lk_ref, lv_ref, s_ref,
    out_ref, held, local, ready, sems, local_sems, out_sems,
):
    _, parts, _, rows, _ = ready.shape
    hd = s_ref.shape[-1]
    copies = [
        fetch((g_ref, v_ref, k_ref), held, sems, hd, h)
        + fetch((lq_ref, lk_ref, lv_ref), local, local_sems, hd, h)
        for h in range(heads)
    ]
    for group in copies:
        for copy in group:
            copy.start()
    first = lax.axis_index("seq") * length
    starts = doc_starts(docs_ref, docs)
    until_here = next_start(starts, first - 1) - first
    from_here = last_start(starts, first + length) - first
    row = lax.broadcasted_iota(jnp.int32, (length, hd), 0)
    offset = row.astype(F32)
    written = []
    for h in range(heads):
        rate = rates_ref[h]
        factor_in = jnp.where(row < until_here, jnp.exp(-rate * (offset + 1.0)), 0.0)
        factor_back = jnp.where(row >= from_here, jnp.exp(-rate * (length - offset)), 0.0)
        matrices = (s_ref[0, h], s_ref[1, h], s_ref[1, h])
        factors = (factor_in, factor_back, factor_back)
        for copy in copies[h]:
            copy.wait()
        for i in range(3):
            outer = dot(held[i, h], matrices[i], 1, 0 if i == 2 else 1) * factors[i]
            grad = (local[i, h] + outer).astype(BF16)
            ready[h, :, i] = grad.reshape(parts, rows, hd)
        written.append(
            pltpu.make_async_copy(
                ready.at[h], out_ref.at[:, :, :, pl.ds(h * hd, hd)], out_sems.at[h]
            )
        )
        written[h].start()
    for copy in written:
        copy.wait()


def spread_kernel(in_ref, *refs):
    outs, sems = refs[:3], refs[3]
    parts, _, _, width = in_ref.shape
    copies = []
    for i in range(3):
        for h in range(parts):
            copy = pltpu.make_async_copy(
                in_ref.at[h, i], outs[i].at[:, pl.ds(h * width, width)], sems.at[i, h]
            )
            copy.start()
            copies.append(copy)
    for copy in copies:
        copy.wait()


def on_chip(array):
    return pltpu.with_memory_space_constraint(array, pltpu.VMEM)


def body(queries, keys, values, grad_out, rates, doc_lengths):
    length, inner = queries.shape
    heads = rates.shape[0]
    docs = doc_lengths.shape[0]
    hd = inner // heads
    blocks = lax.axis_size("seq")
    parts = lax.axis_size("head")
    rows = length // parts
    smem = pl.BlockSpec(memory_space=pltpu.SMEM)
    per_head = pl.BlockSpec((length, hd), lambda h: (0, h))
    anywhere = pl.BlockSpec(memory_space=pl.ANY)
    vmem = pl.BlockSpec(memory_space=pltpu.VMEM)
    summary = pl.pallas_call(
        functools.partial(summary_kernel, length, docs, heads),
        in_specs=[smem, smem] + [anywhere] * 4,
        out_specs=vmem,
        out_shape=jax.ShapeDtypeStruct((2, heads, hd, hd), F32),
        scratch_shapes=[
            pltpu.VMEM((4, heads, length, hd), BF16),
            pltpu.SemaphoreType.DMA((4, heads)),
        ],
        name="summary",
    )(rates, doc_lengths, keys, values, queries, grad_out)
    piece = 2 * heads * hd // blocks
    swapped = lax.all_to_all(
        summary.reshape(blocks, piece, hd), "seq", split_axis=0, concat_axis=0, tiled=True
    )
    *local, keep = pl.pallas_call(
        functools.partial(local_kernel, length, docs, heads, blocks),
        grid=(heads,),
        in_specs=[smem, smem] + [per_head] * 4,
        out_specs=[per_head] * 3
        + [pl.BlockSpec((blocks, hd), lambda h: (0, 0))],
        out_shape=[jax.ShapeDtypeStruct((length, inner), F32)] * 3
        + [jax.ShapeDtypeStruct((blocks, hd), F32)],
        name="local",
    )(rates, doc_lengths, queries, keys, values, grad_out)
    scanned = pl.pallas_call(
        functools.partial(scan_kernel, blocks),
        in_specs=[vmem, vmem],
        out_specs=vmem,
        out_shape=jax.ShapeDtypeStruct((blocks, piece, hd), BF16),
        compiler_params=pltpu.CompilerParams(vmem_limit_bytes=4 << 20),
        name="scan",
    )(keep, on_chip(swapped))
    returned = lax.all_to_all(scanned, "seq", split_axis=0, concat_axis=0, tiled=True)
    grads = pl.pallas_call(
        functools.partial(final_kernel, length, docs, heads),
        in_specs=[smem, smem] + [anywhere] * 6 + [vmem],
        out_specs=anywhere,
        out_shape=jax.ShapeDtypeStruct((parts, 3, rows, inner), BF16),
        scratch_shapes=[
            pltpu.VMEM((3, heads, length, hd), BF16),
            pltpu.VMEM((3, heads, length, hd), F32),
            pltpu.VMEM((heads, parts, 3, rows, hd), BF16),
            pltpu.SemaphoreType.DMA((3, heads)),
            pltpu.SemaphoreType.DMA((3, heads)),
            pltpu.SemaphoreType.DMA((heads,)),
        ],
        name="final",
    )(
        rates, doc_lengths, grad_out, values, keys, *local,
        on_chip(returned.reshape(2, heads, hd, hd)),
    )
    moved = lax.all_to_all(
        grads.reshape(parts, 3 * rows, inner), "head", split_axis=0, concat_axis=0, tiled=True
    ).reshape(parts, 3, rows, inner)
    return pl.pallas_call(
        spread_kernel,
        in_specs=[pl.BlockSpec(memory_space=pl.ANY)],
        out_specs=[pl.BlockSpec(memory_space=pl.ANY)] * 3,
        out_shape=[jax.ShapeDtypeStruct((rows, parts * inner), BF16)] * 3,
        scratch_shapes=[pltpu.SemaphoreType.DMA((3, parts))],
        compiler_params=pltpu.CompilerParams(vmem_limit_bytes=4 << 20),
        name="spread",
    )(moved)


def solution(mesh):
    return jax.shard_map(
        body,
        mesh=mesh,
        in_specs=(
            P("seq", "head"),
            P("seq", "head"),
            P("seq", "head"),
            P("seq", "head"),
            P("head"),
            P(),
        ),
        out_specs=(P(("seq", "head"), None), P(("seq", "head"), None), P(("seq", "head"), None)),
        check_vma=False,
    )
```

```python
import functools

import jax
import jax.numpy as jnp
from jax import lax
from jax.experimental import pallas as pl
from jax.experimental.pallas import tpu as pltpu
from jax.sharding import PartitionSpec as P

BF16 = jnp.bfloat16
F32 = jnp.float32
FAR = 1 << 30


def doc_starts(docs_ref, docs):
    starts = [jnp.int32(0)]
    for i in range(docs - 1):
        starts.append(starts[-1] + docs_ref[i])
    return starts


def last_start(starts, position):
    found = jnp.int32(-1)
    for s in starts:
        found = jnp.maximum(found, jnp.where(s <= position, s, -1))
    return found


def next_start(starts, position):
    found = jnp.int32(FAR)
    for s in starts:
        found = jnp.minimum(found, jnp.where(s > position, s, FAR))
    return found


def dot(a, b, da, db):
    return lax.dot_general(a, b, (((da,), (db,)), ((), ())), preferred_element_type=F32)


def start_all(copies):
    for copy in copies:
        copy.start()


def fetch(refs, buffers, sems):
    return [
        pltpu.make_async_copy(ref, buffer, sems.at[i])
        for i, (ref, buffer) in enumerate(zip(refs, buffers))
    ]


def summary_kernel(
    length, docs, heads,
    rates_hbm, docs_hbm, k_hbm, v_hbm, q_hbm, g_hbm, sums,
    rates_ref, docs_ref, held, sems,
):
    hd = sums.shape[-1]
    copies = fetch(
        (docs_hbm, rates_hbm, k_hbm, v_hbm, q_hbm, g_hbm),
        (docs_ref, rates_ref, *(held.at[i] for i in range(4))),
        sems,
    )
    start_all(copies)
    copies[0].wait()
    first = lax.axis_index("seq") * length
    starts = doc_starts(docs_ref, docs)
    from_here = last_start(starts, first + length - 1) - first
    until_here = next_start(starts, first) - first
    token = lax.broadcasted_iota(jnp.int32, (1, length), 1)
    offset = token.astype(F32)
    copies[1].wait()
    for way in range(2):
        copies[2 + 2 * way].wait()
        copies[3 + 2 * way].wait()
        for h in range(heads):
            at = slice(h * hd, (h + 1) * hd)
            rate = rates_ref[h]
            if way == 0:
                decayed = jnp.exp(-rate * (length - 1.0 - offset))
                weight = jnp.where(token >= from_here, decayed, 0.0)
            else:
                weight = jnp.where(token < until_here, jnp.exp(-rate * offset), 0.0)
            weighted = (held[2 * way, :, at].T.astype(F32) * weight).astype(BF16)
            sums[way, h] = dot(weighted, held[2 * way + 1, :, at], 1, 0)
def local_kernel(
    length, docs, heads, blocks,
    rates_ref, docs_ref, q_ref, k_ref, v_ref, g_ref,
    lq_ref, lk_ref, lv_ref, keep_ref,
):
    head = pl.program_id(0)
    rate = rates_ref[head]
    first = lax.axis_index("seq") * length
    starts = doc_starts(docs_ref, docs)
    t = lax.broadcasted_iota(jnp.int32, (length, length), 0)
    u = lax.broadcasted_iota(jnp.int32, (length, length), 1)
    column = lax.broadcasted_iota(jnp.int32, (length, 1), 0)
    own = jnp.full((length, 1), -FAR, jnp.int32)
    for s in starts:
        here = s - first
        own = jnp.maximum(own, jnp.where(column >= here, here, -FAR))
    distance = (t - u).astype(F32)
    allowed = (u >= own) & (u <= t)
    decayed = jnp.where(allowed, jnp.exp(-rate * jnp.maximum(distance, 0.0)), 0.0)
    q, k, v, g = q_ref[...], k_ref[...], v_ref[...], g_ref[...]
    weights_p = (decayed * dot(g, v, 1, 1)).astype(BF16)
    lq_ref[...] = dot(weights_p, k, 1, 0)
    lk_ref[...] = dot(weights_p, q, 0, 0)
    weights_a = (decayed * dot(q, k, 1, 1)).astype(BF16)
    lv_ref[...] = dot(weights_a, g, 0, 0)

    @pl.when(head == 0)
    def _():
        me = lax.axis_index("seq")
        per_way = blocks // 2
        backward = me // per_way
        mine = rates_ref[(me % per_way) // (per_way // heads)]
        low = lax.broadcasted_iota(jnp.int32, keep_ref.shape, 0) * length + backward
        broken = low < 0
        for s in starts:
            broken = broken | ((s >= low) & (s < low + length))
        decay = jnp.exp(jnp.full(keep_ref.shape, -mine * length, F32))
        keep_ref[...] = jnp.where(broken, 0.0, decay)


def scan_kernel(blocks, keep_ref, in_ref, out_ref):
    backward = lax.axis_index("seq") // (blocks // 2)
    carry = jnp.zeros(in_ref.shape[1:], F32)
    for i in range(blocks):
        j = jnp.where(backward == 1, blocks - 1 - i, i)
        out_ref[j] = carry.astype(BF16)
        carry = keep_ref[pl.ds(j, 1), :] * carry + in_ref[j]


def final_kernel(
    length, docs, heads,
    rates_hbm, docs_hbm, g_hbm, v_hbm, k_hbm, lq_hbm, lk_hbm, lv_hbm, s_ref, out_ref,
    rates_ref, docs_ref, held, local, factors, sems,
):
    parts, _, rows, _ = out_ref.shape
    hd = s_ref.shape[-1]
    copies = fetch(
        (docs_hbm, rates_hbm, g_hbm, lq_hbm, v_hbm, lk_hbm, k_hbm, lv_hbm),
        (docs_ref, rates_ref) + sum(((held.at[i], local.at[i]) for i in range(3)), ()),
        sems,
    )
    start_all(copies)
    copies[0].wait()
    first = lax.axis_index("seq") * length
    starts = doc_starts(docs_ref, docs)
    until_here = next_start(starts, first - 1) - first
    from_here = last_start(starts, first + length) - first
    group = 64
    row = lax.broadcasted_iota(jnp.int32, (group, hd), 0)
    near = row.astype(F32)
    copies[1].wait()
    for h in range(heads):
        rate = rates_ref[h]
        ahead = jnp.exp(-rate * (near + 1.0))
        behind = jnp.exp(-rate * (group - near))
        for low in range(0, length, group):
            these = slice(low, low + group)
            far = jnp.exp(jnp.full((1, hd), -rate * low, F32))
            factors[0, h, these] = jnp.where(row < until_here - low, ahead * far, 0.0)
            far = jnp.exp(jnp.full((1, hd), -rate * (length - group - low), F32))
            factors[1, h, these] = jnp.where(row >= from_here - low, behind * far, 0.0)

    size = length // 1
    for i in range(3):
        copies[2 + 2 * i].wait()
        copies[3 + 2 * i].wait()
        for h in range(heads):
            at = slice(h * hd, (h + 1) * hd)
            matrix = s_ref[min(i, 1), h]
            for low in range(0, length, size):
                these = slice(low, low + size)
                outer = dot(held[i, these, at], matrix, 1, 0 if i == 2 else 1)
                grad = local[i, these, at] + outer * factors[min(i, 1), h, these]
                into = slice(low // rows, (low + size) // rows)
                out_ref[into, i, :, at] = grad.astype(BF16).reshape(size // rows, rows, hd)


def spread_kernel(in_ref, *refs):
    outs, sems = refs[:3], refs[3]
    parts, _, _, width = in_ref.shape
    copies = []
    for i in range(3):
        for h in range(parts):
            copy = pltpu.make_async_copy(
                in_ref.at[h, i], outs[i].at[:, pl.ds(h * width, width)], sems.at[i, h]
            )
            copy.start()
            copies.append(copy)
    for copy in copies:
        copy.wait()


def on_chip(array):
    return pltpu.with_memory_space_constraint(array, pltpu.VMEM)


def body(queries, keys, values, grad_out, rates, doc_lengths):
    length, inner = queries.shape
    heads = rates.shape[0]
    docs = doc_lengths.shape[0]
    hd = inner // heads
    blocks = lax.axis_size("seq")
    parts = lax.axis_size("head")
    rows = length // parts
    smem = pl.BlockSpec(memory_space=pltpu.SMEM)
    per_head = pl.BlockSpec((length, hd), lambda h: (0, h))
    anywhere = pl.BlockSpec(memory_space=pl.ANY)
    vmem = pl.BlockSpec(memory_space=pltpu.VMEM)
    summary = pl.pallas_call(
        functools.partial(summary_kernel, length, docs, heads),
        in_specs=[anywhere] * 6,
        out_specs=vmem,
        out_shape=pltpu.VMEM((2, heads, hd, hd), F32),
        scratch_shapes=[
            pltpu.SMEM((heads,), F32),
            pltpu.SMEM((docs,), jnp.int32),
            pltpu.VMEM((4, length, inner), BF16),
            pltpu.SemaphoreType.DMA((6,)),
        ],
        name="summary",
    )(rates, doc_lengths, keys, values, queries, grad_out)
    piece = 2 * heads * hd // blocks
    swapped = lax.all_to_all(
        summary.reshape(blocks, piece, hd), "seq", split_axis=0, concat_axis=0, tiled=True
    )
    *local, keep = pl.pallas_call(
        functools.partial(local_kernel, length, docs, heads, blocks),
        grid=(heads,),
        in_specs=[smem, smem] + [per_head] * 4,
        out_specs=[per_head] * 3
        + [pl.BlockSpec((blocks, hd), lambda h: (0, 0))],
        out_shape=[jax.ShapeDtypeStruct((length, inner), F32)] * 3
        + [pltpu.VMEM((blocks, hd), F32)],
        name="local",
    )(rates, doc_lengths, queries, keys, values, grad_out)
    scanned = pl.pallas_call(
        functools.partial(scan_kernel, blocks),
        in_specs=[vmem, vmem],
        out_specs=vmem,
        out_shape=jax.ShapeDtypeStruct((blocks, piece, hd), BF16),
        compiler_params=pltpu.CompilerParams(vmem_limit_bytes=4 << 20),
        name="scan",
    )(on_chip(keep), on_chip(swapped))
    returned = lax.all_to_all(scanned, "seq", split_axis=0, concat_axis=0, tiled=True)
    grads = pl.pallas_call(
        functools.partial(final_kernel, length, docs, heads),
        in_specs=[anywhere] * 8 + [vmem],
        out_specs=vmem,
        out_shape=pltpu.VMEM((parts, 3, rows, inner), BF16),
        scratch_shapes=[
            pltpu.SMEM((heads,), F32),
            pltpu.SMEM((docs,), jnp.int32),
            pltpu.VMEM((3, length, inner), BF16),
            pltpu.VMEM((3, length, inner), F32),
            pltpu.VMEM((2, heads, length, hd), F32),
            pltpu.SemaphoreType.DMA((8,)),
        ],
        name="final",
    )(
        rates, doc_lengths, grad_out, values, keys, *local,
        on_chip(returned.reshape(2, heads, hd, hd)),
    )
    moved = lax.all_to_all(
        grads.reshape(parts, 3 * rows, inner), "head", split_axis=0, concat_axis=0, tiled=True
    ).reshape(parts, 3, rows, inner)
    return pl.pallas_call(
        spread_kernel,
        in_specs=[pl.BlockSpec(memory_space=pl.ANY)],
        out_specs=[pl.BlockSpec(memory_space=pl.ANY)] * 3,
        out_shape=[jax.ShapeDtypeStruct((rows, parts * inner), BF16)] * 3,
        scratch_shapes=[pltpu.SemaphoreType.DMA((3, parts))],
        compiler_params=pltpu.CompilerParams(vmem_limit_bytes=4 << 20),
        name="spread",
    )(moved)


def solution(mesh):
    return jax.shard_map(
        body,
        mesh=mesh,
        in_specs=(
            P("seq", "head"),
            P("seq", "head"),
            P("seq", "head"),
            P("seq", "head"),
            P("head"),
            P(),
        ),
        out_specs=(P(("seq", "head"), None), P(("seq", "head"), None), P(("seq", "head"), None)),
        check_vma=False,
    )
```

```python
import functools

import jax
import jax.numpy as jnp
from jax import lax
from jax.experimental import pallas as pl
from jax.experimental.pallas import tpu as pltpu
from jax.sharding import PartitionSpec as P

BF16 = jnp.bfloat16
F32 = jnp.float32
FAR = 1 << 30
LEAD = 11


def doc_starts(docs_ref, docs):
    starts = [jnp.int32(0)]
    for i in range(docs - 1):
        starts.append(starts[-1] + docs_ref[i])
    return starts


def last_start(starts, position):
    found = jnp.int32(-1)
    for s in starts:
        found = jnp.maximum(found, jnp.where(s <= position, s, -1))
    return found


def next_start(starts, position):
    found = jnp.int32(FAR)
    for s in starts:
        found = jnp.minimum(found, jnp.where(s > position, s, FAR))
    return found


def dot(a, b, da, db):
    return lax.dot_general(a, b, (((da,), (db,)), ((), ())), preferred_element_type=F32)


def start_all(copies):
    for copy in copies:
        copy.start()


def fetch(refs, buffers, sems):
    return [
        pltpu.make_async_copy(ref, buffer, sems.at[i])
        for i, (ref, buffer) in enumerate(zip(refs, buffers))
    ]


def summary_kernel(
    length, docs, heads,
    rates_hbm, docs_hbm, k_hbm, v_hbm, q_hbm, g_hbm, sums,
    rates_ref, docs_ref, held, sems,
):
    hd = sums.shape[-1]
    copies = fetch(
        (docs_hbm, rates_hbm, k_hbm, v_hbm, q_hbm, g_hbm),
        (docs_ref, rates_ref, *(held.at[i] for i in range(4))),
        sems,
    )
    start_all(copies)
    copies[0].wait()
    first = lax.axis_index("seq") * length
    starts = doc_starts(docs_ref, docs)
    from_here = last_start(starts, first + length - 1) - first
    until_here = next_start(starts, first) - first
    token = lax.broadcasted_iota(jnp.int32, (1, length), 1)
    offset = token.astype(F32)
    copies[1].wait()
    for way in range(2):
        copies[2 + 2 * way].wait()
        copies[3 + 2 * way].wait()
        for h in range(heads):
            at = slice(h * hd, (h + 1) * hd)
            rate = rates_ref[h]
            if way == 0:
                decayed = jnp.exp(-rate * (length - 1.0 - offset))
                weight = jnp.where(token >= from_here, decayed, 0.0)
            else:
                weight = jnp.where(token < until_here, jnp.exp(-rate * offset), 0.0)
            weighted = (held[2 * way, :, at].T.astype(F32) * weight).astype(BF16)
            sums[way, h] = dot(weighted, held[2 * way + 1, :, at], 1, 0)
def local_kernel(
    length, docs, heads, blocks,
    rates_ref, docs_ref, q_ref, k_ref, v_ref, g_ref,
    lq_ref, lk_ref, lv_ref, keep_ref,
):
    head = pl.program_id(0)
    rate = rates_ref[head]
    first = lax.axis_index("seq") * length
    starts = doc_starts(docs_ref, docs)
    q, k, v, g = q_ref[...], k_ref[...], v_ref[...], g_ref[...]
    half = length // 2
    for low in (0, half):
        rows, seen = slice(low, low + half), slice(0, low + half)
        t = lax.broadcasted_iota(jnp.int32, (half, low + half), 0) + low
        u = lax.broadcasted_iota(jnp.int32, (half, low + half), 1)
        column = lax.broadcasted_iota(jnp.int32, (half, 1), 0) + low
        own = jnp.full((half, 1), -FAR, jnp.int32)
        for s in starts:
            here = s - first
            own = jnp.maximum(own, jnp.where(column >= here, here, -FAR))
        distance = (t - u).astype(F32)
        allowed = (u >= own) & (u <= t)
        decayed = jnp.where(allowed, jnp.exp(-rate * jnp.maximum(distance, 0.0)), 0.0)
        weights_p = (decayed * dot(g[rows], v[seen], 1, 1)).astype(BF16)
        weights_a = (decayed * dot(q[rows], k[seen], 1, 1)).astype(BF16)
        lq_ref[rows] = dot(weights_p, k[seen], 1, 0)
        part_k = dot(weights_p, q[rows], 0, 0)
        part_v = dot(weights_a, g[rows], 0, 0)
        if low:
            lk_ref[:half] = lk_ref[:half] + part_k[:half]
            lk_ref[half:] = part_k[half:]
            lv_ref[:half] = lv_ref[:half] + part_v[:half]
            lv_ref[half:] = part_v[half:]
        else:
            lk_ref[:half] = part_k
            lv_ref[:half] = part_v

    @pl.when(head == 0)
    def _():
        me = lax.axis_index("seq")
        per_way = blocks // 2
        backward = me // per_way
        mine = rates_ref[(me % per_way) // (per_way // heads)]
        low = lax.broadcasted_iota(jnp.int32, keep_ref.shape, 0) * length + backward
        broken = low < 0
        for s in starts:
            broken = broken | ((s >= low) & (s < low + length))
        decay = jnp.exp(jnp.full(keep_ref.shape, -mine * length, F32))
        keep_ref[...] = jnp.where(broken, 0.0, decay)


def scan_kernel(blocks, keep_ref, in_ref, out_ref):
    backward = lax.axis_index("seq") // (blocks // 2)
    carry = jnp.zeros(in_ref.shape[1:], F32)
    for i in range(blocks):
        j = jnp.where(backward == 1, blocks - 1 - i, i)
        out_ref[j] = carry.astype(BF16)
        carry = keep_ref[pl.ds(j, 1), :] * carry + in_ref[j]


def final_kernel(
    length, docs, heads, lead,
    rates_hbm, docs_hbm, g_hbm, v_hbm, k_hbm, lq_hbm, lk_hbm, lv_hbm, s_ref, out_ref,
    rates_ref, docs_ref, held, local, factors, sems,
):
    parts, _, rows, _ = out_ref.shape
    hd = s_ref.shape[-1]
    copies = fetch(
        (docs_hbm, rates_hbm, g_hbm, lq_hbm, v_hbm, lk_hbm, k_hbm, lv_hbm),
        (docs_ref, rates_ref) + sum(((held.at[i], local.at[i]) for i in range(3)), ()),
        sems,
    )
    start_all(copies)
    copies[0].wait()
    first = lax.axis_index("seq") * length
    starts = doc_starts(docs_ref, docs)
    until_here = next_start(starts, first - 1) - first
    from_here = last_start(starts, first + length) - first
    group = 64
    row = lax.broadcasted_iota(jnp.int32, (group, hd), 0)
    near = row.astype(F32)
    copies[1].wait()
    for h in range(heads):
        rate = rates_ref[h]
        ahead = jnp.exp(-rate * (near + 1.0))
        behind = jnp.exp(-rate * (group - near))
        for low in range(0, length, group):
            these = slice(low, low + group)
            far = jnp.exp(jnp.full((1, hd), -rate * low, F32))
            factors[0, h, these] = jnp.where(row < until_here - low, ahead * far, 0.0)
            far = jnp.exp(jnp.full((1, hd), -rate * (length - group - low), F32))
            factors[1, h, these] = jnp.where(row >= from_here - low, behind * far, 0.0)

    for i in range(3):
        copies[2 + 2 * i].wait()
        copies[3 + 2 * i].wait()
        for h in range(heads):
            at = slice(h * hd, (h + 1) * hd)
            matrix = s_ref[min(i, 1), h]
            outer = dot(held[i, :, at], matrix, 1, 0 if i == 2 else 1)
            grad = (local[i, :, at] + outer * factors[min(i, 1), h]).astype(BF16)
            grad = grad.reshape(parts, rows, hd)
            out_ref[: parts - lead, i, :, at] = grad[lead:]
            out_ref[parts - lead :, i, :, at] = grad[:lead]


def spread_kernel(lead, in_ref, *refs):
    outs, sems = refs[:3], refs[3]
    parts, _, _, width = in_ref.shape
    copies = []
    for i in range(3):
        for h in range(parts):
            column = (h + lead) % parts * width
            copy = pltpu.make_async_copy(
                in_ref.at[h, i], outs[i].at[:, pl.ds(column, width)], sems.at[i, h]
            )
            copy.start()
            copies.append(copy)
    for copy in copies:
        copy.wait()


def on_chip(array):
    return pltpu.with_memory_space_constraint(array, pltpu.VMEM)


def body(queries, keys, values, grad_out, rates, doc_lengths):
    length, inner = queries.shape
    heads = rates.shape[0]
    docs = doc_lengths.shape[0]
    hd = inner // heads
    blocks = lax.axis_size("seq")
    parts = lax.axis_size("head")
    rows = length // parts
    lead = LEAD % parts
    smem = pl.BlockSpec(memory_space=pltpu.SMEM)
    per_head = pl.BlockSpec((length, hd), lambda h: (0, h))
    anywhere = pl.BlockSpec(memory_space=pl.ANY)
    vmem = pl.BlockSpec(memory_space=pltpu.VMEM)
    summary = pl.pallas_call(
        functools.partial(summary_kernel, length, docs, heads),
        in_specs=[anywhere] * 6,
        out_specs=vmem,
        out_shape=pltpu.VMEM((2, heads, hd, hd), F32),
        scratch_shapes=[
            pltpu.SMEM((heads,), F32),
            pltpu.SMEM((docs,), jnp.int32),
            pltpu.VMEM((4, length, inner), BF16),
            pltpu.SemaphoreType.DMA((6,)),
        ],
        name="summary",
    )(rates, doc_lengths, keys, values, queries, grad_out)
    piece = 2 * heads * hd // blocks
    swapped = lax.all_to_all(
        summary.reshape(blocks, piece, hd), "seq", split_axis=0, concat_axis=0, tiled=True
    )
    *local, keep = pl.pallas_call(
        functools.partial(local_kernel, length, docs, heads, blocks),
        grid=(heads,),
        in_specs=[smem, smem] + [per_head] * 4,
        out_specs=[per_head] * 3
        + [pl.BlockSpec((blocks, hd), lambda h: (0, 0))],
        out_shape=[jax.ShapeDtypeStruct((length, inner), F32)] * 3
        + [pltpu.VMEM((blocks, hd), F32)],
        name="local",
    )(rates, doc_lengths, queries, keys, values, grad_out)
    scanned = pl.pallas_call(
        functools.partial(scan_kernel, blocks),
        in_specs=[vmem, vmem],
        out_specs=vmem,
        out_shape=jax.ShapeDtypeStruct((blocks, piece, hd), BF16),
        compiler_params=pltpu.CompilerParams(vmem_limit_bytes=4 << 20),
        name="scan",
    )(on_chip(keep), on_chip(swapped))
    returned = lax.all_to_all(scanned, "seq", split_axis=0, concat_axis=0, tiled=True)
    grads = pl.pallas_call(
        functools.partial(final_kernel, length, docs, heads, lead),
        in_specs=[anywhere] * 8 + [vmem],
        out_specs=vmem,
        out_shape=pltpu.VMEM((parts, 3, rows, inner), BF16),
        scratch_shapes=[
            pltpu.SMEM((heads,), F32),
            pltpu.SMEM((docs,), jnp.int32),
            pltpu.VMEM((3, length, inner), BF16),
            pltpu.VMEM((3, length, inner), F32),
            pltpu.VMEM((2, heads, length, hd), F32),
            pltpu.SemaphoreType.DMA((8,)),
        ],
        name="final",
    )(
        rates, doc_lengths, grad_out, values, keys, *local,
        on_chip(returned.reshape(2, heads, hd, hd)),
    )
    moved = lax.all_to_all(
        grads.reshape(parts, 3 * rows, inner),
        "head",
        split_axis=0,
        concat_axis=0,
        axis_index_groups=[[(lead + p) % parts for p in range(parts)]],
        tiled=True,
    ).reshape(parts, 3, rows, inner)
    return pl.pallas_call(
        functools.partial(spread_kernel, lead),
        in_specs=[pl.BlockSpec(memory_space=pl.ANY)],
        out_specs=[pl.BlockSpec(memory_space=pl.ANY)] * 3,
        out_shape=[jax.ShapeDtypeStruct((rows, parts * inner), BF16)] * 3,
        scratch_shapes=[pltpu.SemaphoreType.DMA((3, parts))],
        compiler_params=pltpu.CompilerParams(vmem_limit_bytes=4 << 20),
        name="spread",
    )(moved)


def solution(mesh):
    return jax.shard_map(
        body,
        mesh=mesh,
        in_specs=(
            P("seq", "head"),
            P("seq", "head"),
            P("seq", "head"),
            P("seq", "head"),
            P("head"),
            P(),
        ),
        out_specs=(P(("seq", "head"), None), P(("seq", "head"), None), P(("seq", "head"), None)),
        check_vma=False,
    )
```

```python
import functools

import jax
import jax.numpy as jnp
from jax import lax
from jax.experimental import pallas as pl
from jax.experimental.pallas import tpu as pltpu
from jax.sharding import PartitionSpec as P

BF16 = jnp.bfloat16
F32 = jnp.float32
FAR = 1 << 30
LEAD = 11


def doc_starts(docs_ref, docs):
    starts = [jnp.int32(0)]
    for i in range(docs - 1):
        starts.append(starts[-1] + docs_ref[i])
    return starts


def last_start(starts, position):
    found = jnp.int32(-1)
    for s in starts:
        found = jnp.maximum(found, jnp.where(s <= position, s, -1))
    return found


def next_start(starts, position):
    found = jnp.int32(FAR)
    for s in starts:
        found = jnp.minimum(found, jnp.where(s > position, s, FAR))
    return found


def dot(a, b, da, db):
    return lax.dot_general(a, b, (((da,), (db,)), ((), ())), preferred_element_type=F32)


def start_all(copies):
    for copy in copies:
        copy.start()


def fetch(refs, buffers, sems):
    return [
        pltpu.make_async_copy(ref, buffer, sems.at[i])
        for i, (ref, buffer) in enumerate(zip(refs, buffers))
    ]


def summary_kernel(
    length, docs, heads,
    rates_hbm, docs_hbm, k_hbm, v_hbm, q_hbm, g_hbm, sums,
    rates_ref, docs_ref, held, sems,
):
    hd = sums.shape[-1]
    copies = fetch(
        (docs_hbm, rates_hbm, k_hbm, v_hbm, q_hbm, g_hbm),
        (docs_ref, rates_ref, *(held.at[i] for i in range(4))),
        sems,
    )
    start_all(copies)
    copies[0].wait()
    first = lax.axis_index("seq") * length
    starts = doc_starts(docs_ref, docs)
    from_here = last_start(starts, first + length - 1) - first
    until_here = next_start(starts, first) - first
    token = lax.broadcasted_iota(jnp.int32, (1, length), 1)
    offset = token.astype(F32)
    copies[1].wait()
    for way in range(2):
        copies[2 + 2 * way].wait()
        copies[3 + 2 * way].wait()
        for h in range(heads):
            at = slice(h * hd, (h + 1) * hd)
            rate = rates_ref[h]
            if way == 0:
                decayed = jnp.exp(-rate * (length - 1.0 - offset))
                weight = jnp.where(token >= from_here, decayed, 0.0)
            else:
                weight = jnp.where(token < until_here, jnp.exp(-rate * offset), 0.0)
            weighted = (held[2 * way, :, at].T.astype(F32) * weight).astype(BF16)
            sums[way, h] = dot(weighted, held[2 * way + 1, :, at], 1, 0)
def local_kernel(
    length, docs, heads, blocks,
    rates_ref, docs_ref, q_ref, k_ref, v_ref, g_ref,
    lq_ref, lk_ref, lv_ref, keep_ref,
):
    head = pl.program_id(0)
    rate = rates_ref[head]
    first = lax.axis_index("seq") * length
    starts = doc_starts(docs_ref, docs)
    q, k, v, g = q_ref[...], k_ref[...], v_ref[...], g_ref[...]
    half = length // 2
    for low in (0, half):
        rows, seen = slice(low, low + half), slice(0, low + half)
        t = lax.broadcasted_iota(jnp.int32, (half, low + half), 0) + low
        u = lax.broadcasted_iota(jnp.int32, (half, low + half), 1)
        column = lax.broadcasted_iota(jnp.int32, (half, 1), 0) + low
        own = jnp.full((half, 1), -FAR, jnp.int32)
        for s in starts:
            here = s - first
            own = jnp.maximum(own, jnp.where(column >= here, here, -FAR))
        distance = (t - u).astype(F32)
        allowed = (u >= own) & (u <= t)
        decayed = jnp.where(allowed, jnp.exp(-rate * jnp.maximum(distance, 0.0)), 0.0)
        weights_p = (decayed * dot(g[rows], v[seen], 1, 1)).astype(BF16)
        weights_a = (decayed * dot(q[rows], k[seen], 1, 1)).astype(BF16)
        lq_ref[rows] = dot(weights_p, k[seen], 1, 0)
        part_k = dot(weights_p, q[rows], 0, 0)
        part_v = dot(weights_a, g[rows], 0, 0)
        if low:
            lk_ref[:half] = lk_ref[:half] + part_k[:half]
            lk_ref[half:] = part_k[half:]
            lv_ref[:half] = lv_ref[:half] + part_v[:half]
            lv_ref[half:] = part_v[half:]
        else:
            lk_ref[:half] = part_k
            lv_ref[:half] = part_v

    @pl.when(head == 0)
    def _():
        me = lax.axis_index("seq")
        per_way = blocks // 2
        backward = me // per_way
        mine = rates_ref[(me % per_way) // (per_way // heads)]
        low = lax.broadcasted_iota(jnp.int32, keep_ref.shape, 0) * length + backward
        broken = low < 0
        for s in starts:
            broken = broken | ((s >= low) & (s < low + length))
        decay = jnp.exp(jnp.full(keep_ref.shape, -mine * length, F32))
        keep_ref[...] = jnp.where(broken, 0.0, decay)


def scan_kernel(blocks, keep_ref, in_ref, out_ref):
    backward = lax.axis_index("seq") // (blocks // 2)
    carry = jnp.zeros(in_ref.shape[1:], F32)
    for i in range(blocks):
        j = jnp.where(backward == 1, blocks - 1 - i, i)
        out_ref[j] = carry.astype(BF16)
        carry = keep_ref[pl.ds(j, 1), :] * carry + in_ref[j]


def final_kernel(
    length, docs, heads, lead,
    rates_hbm, docs_hbm, lq_hbm, lk_hbm, lv_hbm, g_ref, v_ref, k_ref, s_ref, out_ref,
    rates_ref, docs_ref, local, factors, sems,
):
    parts, _, rows, _ = out_ref.shape
    hd = s_ref.shape[-1]
    copies = fetch(
        (docs_hbm, rates_hbm, lq_hbm, lk_hbm, lv_hbm),
        (docs_ref, rates_ref, *(local.at[i] for i in range(3))),
        sems,
    )
    start_all(copies)
    copies[0].wait()
    first = lax.axis_index("seq") * length
    starts = doc_starts(docs_ref, docs)
    until_here = next_start(starts, first - 1) - first
    from_here = last_start(starts, first + length) - first
    group = 64
    row = lax.broadcasted_iota(jnp.int32, (group, hd), 0)
    near = row.astype(F32)
    copies[1].wait()
    for h in range(heads):
        rate = rates_ref[h]
        ahead = jnp.exp(-rate * (near + 1.0))
        behind = jnp.exp(-rate * (group - near))
        for low in range(0, length, group):
            these = slice(low, low + group)
            far = jnp.exp(jnp.full((1, hd), -rate * low, F32))
            factors[0, h, these] = jnp.where(row < until_here - low, ahead * far, 0.0)
            far = jnp.exp(jnp.full((1, hd), -rate * (length - group - low), F32))
            factors[1, h, these] = jnp.where(row >= from_here - low, behind * far, 0.0)

    for i, rows_ref in enumerate((g_ref, v_ref, k_ref)):
        copies[2 + i].wait()
        for h in range(heads):
            at = slice(h * hd, (h + 1) * hd)
            matrix = s_ref[min(i, 1), h]
            outer = dot(rows_ref[:, at], matrix, 1, 0 if i == 2 else 1)
            grad = (local[i, :, at] + outer * factors[min(i, 1), h]).astype(BF16)
            grad = grad.reshape(parts, rows, hd)
            out_ref[: parts - lead, i, :, at] = grad[lead:]
            out_ref[parts - lead :, i, :, at] = grad[:lead]


def spread_kernel(lead, in_ref, *refs):
    outs, sems = refs[:3], refs[3]
    parts, _, _, width = in_ref.shape
    copies = []
    for i in range(3):
        for h in range(parts):
            column = (h + lead) % parts * width
            copy = pltpu.make_async_copy(
                in_ref.at[h, i], outs[i].at[:, pl.ds(column, width)], sems.at[i, h]
            )
            copy.start()
            copies.append(copy)
    for copy in copies:
        copy.wait()


def on_chip(array):
    return pltpu.with_memory_space_constraint(array, pltpu.VMEM)


def body(queries, keys, values, grad_out, rates, doc_lengths):
    length, inner = queries.shape
    heads = rates.shape[0]
    docs = doc_lengths.shape[0]
    hd = inner // heads
    blocks = lax.axis_size("seq")
    parts = lax.axis_size("head")
    rows = length // parts
    lead = LEAD % parts
    smem = pl.BlockSpec(memory_space=pltpu.SMEM)
    per_head = pl.BlockSpec((length, hd), lambda h: (0, h))
    anywhere = pl.BlockSpec(memory_space=pl.ANY)
    vmem = pl.BlockSpec(memory_space=pltpu.VMEM)
    summary = pl.pallas_call(
        functools.partial(summary_kernel, length, docs, heads),
        in_specs=[anywhere] * 6,
        out_specs=vmem,
        out_shape=pltpu.VMEM((2, heads, hd, hd), F32),
        scratch_shapes=[
            pltpu.SMEM((heads,), F32),
            pltpu.SMEM((docs,), jnp.int32),
            pltpu.VMEM((4, length, inner), BF16),
            pltpu.SemaphoreType.DMA((6,)),
        ],
        name="summary",
    )(rates, doc_lengths, keys, values, queries, grad_out)
    piece = 2 * heads * hd // blocks
    swapped = lax.all_to_all(
        summary.reshape(blocks, piece, hd), "seq", split_axis=0, concat_axis=0, tiled=True
    )
    *local, keep = pl.pallas_call(
        functools.partial(local_kernel, length, docs, heads, blocks),
        grid=(heads,),
        in_specs=[smem, smem] + [per_head] * 4,
        out_specs=[per_head] * 3
        + [pl.BlockSpec((blocks, hd), lambda h: (0, 0))],
        out_shape=[jax.ShapeDtypeStruct((length, inner), F32)] * 3
        + [pltpu.VMEM((blocks, hd), F32)],
        name="local",
    )(rates, doc_lengths, queries, keys, values, grad_out)
    scanned = pl.pallas_call(
        functools.partial(scan_kernel, blocks),
        in_specs=[vmem, vmem],
        out_specs=vmem,
        out_shape=jax.ShapeDtypeStruct((blocks, piece, hd), BF16),
        compiler_params=pltpu.CompilerParams(vmem_limit_bytes=4 << 20),
        name="scan",
    )(on_chip(keep), on_chip(swapped))
    returned = lax.all_to_all(scanned, "seq", split_axis=0, concat_axis=0, tiled=True)
    grads = pl.pallas_call(
        functools.partial(final_kernel, length, docs, heads, lead),
        in_specs=[anywhere] * 5 + [vmem] * 4,
        out_specs=vmem,
        out_shape=pltpu.VMEM((parts, 3, rows, inner), BF16),
        scratch_shapes=[
            pltpu.SMEM((heads,), F32),
            pltpu.SMEM((docs,), jnp.int32),
            pltpu.VMEM((3, length, inner), F32),
            pltpu.VMEM((2, heads, length, hd), F32),
            pltpu.SemaphoreType.DMA((5,)),
        ],
        name="final",
    )(
        rates, doc_lengths, *local,
        *[on_chip(a) for a in (grad_out, values, keys)],
        on_chip(returned.reshape(2, heads, hd, hd)),
    )
    moved = lax.all_to_all(
        grads.reshape(parts, 3 * rows, inner),
        "head",
        split_axis=0,
        concat_axis=0,
        axis_index_groups=[[(lead + p) % parts for p in range(parts)]],
        tiled=True,
    ).reshape(parts, 3, rows, inner)
    return pl.pallas_call(
        functools.partial(spread_kernel, lead),
        in_specs=[pl.BlockSpec(memory_space=pl.ANY)],
        out_specs=[pl.BlockSpec(memory_space=pl.ANY)] * 3,
        out_shape=[jax.ShapeDtypeStruct((rows, parts * inner), BF16)] * 3,
        scratch_shapes=[pltpu.SemaphoreType.DMA((3, parts))],
        compiler_params=pltpu.CompilerParams(vmem_limit_bytes=4 << 20),
        name="spread",
    )(moved)


def solution(mesh):
    return jax.shard_map(
        body,
        mesh=mesh,
        in_specs=(
            P("seq", "head"),
            P("seq", "head"),
            P("seq", "head"),
            P("seq", "head"),
            P("head"),
            P(),
        ),
        out_specs=(P(("seq", "head"), None), P(("seq", "head"), None), P(("seq", "head"), None)),
        check_vma=False,
    )
```

```python
import functools

import jax
import jax.numpy as jnp
from jax import lax
from jax.experimental import pallas as pl
from jax.experimental.pallas import tpu as pltpu
from jax.sharding import PartitionSpec as P

BF16 = jnp.bfloat16
F32 = jnp.float32
FAR = 1 << 30
LEAD = 11


def doc_starts(docs_ref, docs):
    starts = [jnp.int32(0)]
    for i in range(docs - 1):
        starts.append(starts[-1] + docs_ref[i])
    return starts


def last_start(starts, position):
    found = jnp.int32(-1)
    for s in starts:
        found = jnp.maximum(found, jnp.where(s <= position, s, -1))
    return found


def next_start(starts, position):
    found = jnp.int32(FAR)
    for s in starts:
        found = jnp.minimum(found, jnp.where(s > position, s, FAR))
    return found


def dot(a, b, da, db):
    return lax.dot_general(a, b, (((da,), (db,)), ((), ())), preferred_element_type=F32)


def start_all(copies):
    for copy in copies:
        copy.start()


def fetch(refs, buffers, sems):
    return [
        pltpu.make_async_copy(ref, buffer, sems.at[i])
        for i, (ref, buffer) in enumerate(zip(refs, buffers))
    ]


def summary_kernel(
    length, docs, heads,
    rates_hbm, docs_hbm, k_hbm, v_hbm, q_hbm, g_hbm, sums,
    rates_ref, docs_ref, held, sems,
):
    hd = sums.shape[-1]
    copies = fetch(
        (docs_hbm, rates_hbm, k_hbm, v_hbm, q_hbm, g_hbm),
        (docs_ref, rates_ref, *(held.at[i] for i in range(4))),
        sems,
    )
    start_all(copies)
    copies[0].wait()
    first = lax.axis_index("seq") * length
    starts = doc_starts(docs_ref, docs)
    from_here = last_start(starts, first + length - 1) - first
    until_here = next_start(starts, first) - first
    token = lax.broadcasted_iota(jnp.int32, (1, length), 1)
    offset = token.astype(F32)
    copies[1].wait()
    for way in range(2):
        copies[2 + 2 * way].wait()
        copies[3 + 2 * way].wait()
        for h in range(heads):
            at = slice(h * hd, (h + 1) * hd)
            rate = rates_ref[h]
            if way == 0:
                decayed = jnp.exp(-rate * (length - 1.0 - offset))
                weight = jnp.where(token >= from_here, decayed, 0.0)
            else:
                weight = jnp.where(token < until_here, jnp.exp(-rate * offset), 0.0)
            weighted = (held[2 * way, :, at].T.astype(F32) * weight).astype(BF16)
            sums[way, h] = dot(weighted, held[2 * way + 1, :, at], 1, 0)
def local_kernel(
    length, docs, heads, blocks,
    rates_ref, docs_ref, q_ref, k_ref, v_ref, g_ref,
    lq_ref, lk_ref, lv_ref, keep_ref,
):
    head = pl.program_id(0)
    rate = rates_ref[head]
    first = lax.axis_index("seq") * length
    starts = doc_starts(docs_ref, docs)
    q, k, v, g = q_ref[...], k_ref[...], v_ref[...], g_ref[...]
    half = length // 2
    for low in (0, half):
        rows, seen = slice(low, low + half), slice(0, low + half)
        t = lax.broadcasted_iota(jnp.int32, (half, low + half), 0) + low
        u = lax.broadcasted_iota(jnp.int32, (half, low + half), 1)
        column = lax.broadcasted_iota(jnp.int32, (half, 1), 0) + low
        own = jnp.full((half, 1), -FAR, jnp.int32)
        for s in starts:
            here = s - first
            own = jnp.maximum(own, jnp.where(column >= here, here, -FAR))
        distance = (t - u).astype(F32)
        allowed = (u >= own) & (u <= t)
        decayed = jnp.where(allowed, jnp.exp(-rate * jnp.maximum(distance, 0.0)), 0.0)
        weights_p = (decayed * dot(g[rows], v[seen], 1, 1)).astype(BF16)
        weights_a = (decayed * dot(q[rows], k[seen], 1, 1)).astype(BF16)
        lq_ref[rows] = dot(weights_p, k[seen], 1, 0)
        part_k = dot(weights_p, q[rows], 0, 0)
        part_v = dot(weights_a, g[rows], 0, 0)
        if low:
            lk_ref[:half] = lk_ref[:half] + part_k[:half]
            lk_ref[half:] = part_k[half:]
            lv_ref[:half] = lv_ref[:half] + part_v[:half]
            lv_ref[half:] = part_v[half:]
        else:
            lk_ref[:half] = part_k
            lv_ref[:half] = part_v

    @pl.when(head == 0)
    def _():
        me = lax.axis_index("seq")
        per_way = blocks // 2
        backward = me // per_way
        mine = rates_ref[(me % per_way) // (per_way // heads)]
        low = lax.broadcasted_iota(jnp.int32, keep_ref.shape, 0) * length + backward
        broken = low < 0
        for s in starts:
            broken = broken | ((s >= low) & (s < low + length))
        decay = jnp.exp(jnp.full(keep_ref.shape, -mine * length, F32))
        keep_ref[...] = jnp.where(broken, 0.0, decay)


def scan_kernel(blocks, keep_ref, in_ref, out_ref):
    backward = lax.axis_index("seq") // (blocks // 2)
    carry = jnp.zeros(in_ref.shape[1:], F32)
    for i in range(blocks):
        j = jnp.where(backward == 1, blocks - 1 - i, i)
        out_ref[j] = carry.astype(BF16)
        carry = keep_ref[pl.ds(j, 1), :] * carry + in_ref[j]


def final_kernel(
    length, docs, heads, lead,
    rates_hbm, docs_hbm, lq_hbm, lk_hbm, lv_hbm, g_ref, v_ref, k_ref, s_ref, out_ref,
    rates_ref, docs_ref, local, factors, sems,
):
    parts, _, rows, _ = out_ref.shape
    hd = s_ref.shape[-1]
    copies = fetch(
        (docs_hbm, rates_hbm, lq_hbm, lk_hbm, lv_hbm),
        (docs_ref, rates_ref, *(local.at[i] for i in range(3))),
        sems,
    )
    start_all(copies)
    copies[0].wait()
    first = lax.axis_index("seq") * length
    starts = doc_starts(docs_ref, docs)
    until_here = next_start(starts, first - 1) - first
    from_here = last_start(starts, first + length) - first
    group = 64
    row = lax.broadcasted_iota(jnp.int32, (group, hd), 0)
    near = row.astype(F32)
    copies[1].wait()
    for h in range(heads):
        rate = rates_ref[h]
        ahead = jnp.exp(-rate * (near + 1.0))
        behind = jnp.exp(-rate * (group - near))
        for low in range(0, length, group):
            these = slice(low, low + group)
            far = jnp.exp(jnp.full((1, hd), -rate * low, F32))
            factors[0, h, these] = jnp.where(row < until_here - low, ahead * far, 0.0)
            far = jnp.exp(jnp.full((1, hd), -rate * (length - group - low), F32))
            factors[1, h, these] = jnp.where(row >= from_here - low, behind * far, 0.0)

    for i, rows_ref in enumerate((g_ref, v_ref, k_ref)):
        copies[2 + i].wait()
        for h in range(heads):
            at = slice(h * hd, (h + 1) * hd)
            matrix = s_ref[min(i, 1), h]
            outer = dot(rows_ref[:, at], matrix, 1, 0 if i == 2 else 1)
            grad = (local[i, :, at] + outer * factors[min(i, 1), h]).astype(BF16)
            grad = grad.reshape(parts, rows, hd)
            out_ref[: parts - lead, i, :, at] = grad[lead:]
            out_ref[parts - lead :, i, :, at] = grad[:lead]


def spread_kernel(lead, in_ref, *refs):
    outs, sems = refs[:3], refs[3]
    parts, _, tiles, _, _ = in_ref.shape
    copies = []
    for i in range(3):
        for r in range(tiles):
            for side, (low, size, to) in enumerate(
                ((0, parts - lead, lead), (parts - lead, lead, 0))
            ):
                copy = pltpu.make_async_copy(
                    in_ref.at[pl.ds(low, size), i, r],
                    outs[i].at[r, pl.ds(to, size)],
                    sems.at[i, r, side],
                )
                copy.start()
                copies.append(copy)
    for copy in copies:
        copy.wait()


def on_chip(array):
    return pltpu.with_memory_space_constraint(array, pltpu.VMEM)


def body(queries, keys, values, grad_out, rates, doc_lengths):
    length, inner = queries.shape
    heads = rates.shape[0]
    docs = doc_lengths.shape[0]
    hd = inner // heads
    blocks = lax.axis_size("seq")
    parts = lax.axis_size("head")
    rows = length // parts
    lead = LEAD % parts
    smem = pl.BlockSpec(memory_space=pltpu.SMEM)
    per_head = pl.BlockSpec((length, hd), lambda h: (0, h))
    anywhere = pl.BlockSpec(memory_space=pl.ANY)
    vmem = pl.BlockSpec(memory_space=pltpu.VMEM)
    summary = pl.pallas_call(
        functools.partial(summary_kernel, length, docs, heads),
        in_specs=[anywhere] * 6,
        out_specs=vmem,
        out_shape=pltpu.VMEM((2, heads, hd, hd), F32),
        scratch_shapes=[
            pltpu.SMEM((heads,), F32),
            pltpu.SMEM((docs,), jnp.int32),
            pltpu.VMEM((4, length, inner), BF16),
            pltpu.SemaphoreType.DMA((6,)),
        ],
        name="summary",
    )(rates, doc_lengths, keys, values, queries, grad_out)
    piece = 2 * heads * hd // blocks
    swapped = lax.all_to_all(
        summary.reshape(blocks, piece, hd), "seq", split_axis=0, concat_axis=0, tiled=True
    )
    *local, keep = pl.pallas_call(
        functools.partial(local_kernel, length, docs, heads, blocks),
        grid=(heads,),
        in_specs=[smem, smem] + [per_head] * 4,
        out_specs=[per_head] * 3
        + [pl.BlockSpec((blocks, hd), lambda h: (0, 0))],
        out_shape=[jax.ShapeDtypeStruct((length, inner), F32)] * 3
        + [pltpu.VMEM((blocks, hd), F32)],
        name="local",
    )(rates, doc_lengths, queries, keys, values, grad_out)
    scanned = pl.pallas_call(
        functools.partial(scan_kernel, blocks),
        in_specs=[vmem, vmem],
        out_specs=vmem,
        out_shape=jax.ShapeDtypeStruct((blocks, piece, hd), BF16),
        compiler_params=pltpu.CompilerParams(vmem_limit_bytes=4 << 20),
        name="scan",
    )(on_chip(keep), on_chip(swapped))
    returned = lax.all_to_all(scanned, "seq", split_axis=0, concat_axis=0, tiled=True)
    grads = pl.pallas_call(
        functools.partial(final_kernel, length, docs, heads, lead),
        in_specs=[anywhere] * 5 + [vmem] * 4,
        out_specs=vmem,
        out_shape=pltpu.VMEM((parts, 3, rows, inner), BF16),
        scratch_shapes=[
            pltpu.SMEM((heads,), F32),
            pltpu.SMEM((docs,), jnp.int32),
            pltpu.VMEM((3, length, inner), F32),
            pltpu.VMEM((2, heads, length, hd), F32),
            pltpu.SemaphoreType.DMA((5,)),
        ],
        name="final",
    )(
        rates, doc_lengths, *local,
        *[on_chip(a) for a in (grad_out, values, keys)],
        on_chip(returned.reshape(2, heads, hd, hd)),
    )
    moved = lax.all_to_all(
        grads.reshape(parts, 3 * rows, inner),
        "head",
        split_axis=0,
        concat_axis=0,
        axis_index_groups=[[(lead + p) % parts for p in range(parts)]],
        tiled=True,
    ).reshape(parts, 3, rows // 8, 8, inner)
    spread = pl.pallas_call(
        functools.partial(spread_kernel, lead),
        in_specs=[anywhere],
        out_specs=[anywhere] * 3,
        out_shape=[jax.ShapeDtypeStruct((rows // 8, parts, 8, inner), BF16)] * 3,
        scratch_shapes=[pltpu.SemaphoreType.DMA((3, rows // 8, 2))],
        compiler_params=pltpu.CompilerParams(vmem_limit_bytes=4 << 20),
        name="spread",
    )(moved)
    return tuple(a.transpose(0, 2, 1, 3).reshape(rows, parts * inner) for a in spread)


def solution(mesh):
    return jax.shard_map(
        body,
        mesh=mesh,
        in_specs=(
            P("seq", "head"),
            P("seq", "head"),
            P("seq", "head"),
            P("seq", "head"),
            P("head"),
            P(),
        ),
        out_specs=(P(("seq", "head"), None), P(("seq", "head"), None), P(("seq", "head"), None)),
        check_vma=False,
    )
```
